512 devices in a mesh: row: 32 (over z, x_lo), col: 16 (over x_hi, y, core).
Axes of the slice: x: 4 (x_hi: 2, x_lo: 2; x = x_hi * 2 + x_lo), y: 4, z: 16, core: 2. Of those that a mesh axis runs over, the one named last changes fastest.
Arguments:
- coupling: float32 [16384, 32, 512], P('col', 'row'), may hold values from -0.125 to 0.125
- lag_class: int32 [16, 32], P('col', 'row'), may hold values from 0 to 1
- rates_older: float32 [16, 32, 32, 2, 128], P('col', 'row'), may hold values from 0.05 to 0.95
- rates_newer: float32 [16, 32, 32, 2, 128], P('col', 'row'), may hold values from 0.05 to 0.95
- drive: float32 [3, 16, 32, 32, 2, 128], P(None, 'col', 'row'), may hold values from -6 to 6
- syn_kernel: float32 [128, 128], replicated, may hold values from 0 to 1, as said below
Outputs:
- rates: float32 [3, 16, 32, 32, 2, 128], P(None, 'col', 'row')
The draws below stay inside these ranges and needn't reach their ends.
Inputs may be any that keep to these rules, and one draw needn't show every extreme that they name: syn_kernel is zero above its diagonal.
All inputs are finite; a program needn't handle non-finite values.
Results may differ from the reference program's by a relative error of at most 0.0001.
Values sent between devices are 32-bit elements; how exact they have to be, the bound alone decides.
A program may use at most 64 MiB of HBM per device.

```python
import jax
import jax.numpy as jnp
from jax import lax

GROUP = 32
RUNS = 2
STEPS = 128
SLABS = 3
NODES = 16384
SRC_BLOCK = 512
N_ROW = 32
N_COL = 16


def draw_syn_kernel(key, part):
    key_diag, key_off, key_tau = jax.random.split(key, 3)
    times = jnp.arange(STEPS)
    lagged = (times[:, None] - times[None, :]).astype(jnp.float32)
    tau = jnp.exp(jax.random.uniform(key_tau, (), jnp.float32, jnp.log(8.0), jnp.log(40.0)))
    factors = jax.random.uniform(key_off, (STEPS, STEPS), jnp.float32, 0.5, 1.5)
    falloff = jnp.exp(-jnp.maximum(lagged, 0.0) / tau)
    lower = jnp.where(lagged > 0, 0.15 * factors * falloff, 0.0)
    diagonal = jax.random.uniform(key_diag, (STEPS,), jnp.float32, 0.6, 1.0)
    return lower + jnp.diag(diagonal)


def plant(entries, own_key, least, high):
    place = [jax.random.randint(jax.random.fold_in(own_key, axis), (), 0, length) for axis, length in enumerate(entries.shape)]
    widest = entries.shape.index(max(entries.shape))
    next_to = place[:widest] + [(place[widest] + 1) % entries.shape[widest]] + place[widest + 1:]
    return entries.at[tuple(place)].set(least).at[tuple(next_to)].set(high)


def block_scale(stream_key, dims, cuts, smallest, largest):
    level, own = 1.0, jax.random.fold_in(stream_key, 6)
    for dim, blocks in cuts:
        steps = jnp.exp(jax.random.uniform(jax.random.fold_in(own, dim), (blocks,), jnp.float32, smallest / len(cuts), largest / len(cuts)))
        level = level * jnp.repeat(steps, dims[dim] // blocks).reshape([-1 if axis == dim else 1 for axis in range(len(dims))])
    return level


def gaussian(key, extent, spread, bound, cuts=(), held_as=jnp.bfloat16):
    level = block_scale(key, extent, cuts, -0.22, 0.18) if cuts else 1.0
    array = jax.random.normal(key, extent, jnp.float32) * spread * level
    return jnp.minimum(jnp.maximum(array, -bound), bound).astype(held_as)


def setup_inputs(seed: int = 0) -> dict:
    key_list = jax.random.split(jax.random.key(seed), 7)
    return {
        "coupling": gaussian(key_list[0], (NODES, N_ROW, SRC_BLOCK), (NODES // 8) ** -0.5, 0.125, ((0, 16), (1, 32)), jnp.float32),
        "lag_class": plant(jax.random.randint(key_list[1], (N_COL, N_ROW), 0, 2), jax.random.fold_in(key_list[1], 1), 0, 1).astype(jnp.int32),
        "rates_older": jnp.clip(0.05 + 0.9 * jax.random.uniform(key_list[2], (N_COL, N_ROW, GROUP, RUNS, STEPS), jnp.float32) ** block_scale(key_list[2], (N_COL, N_ROW, GROUP, RUNS, STEPS), ((0, 16), (1, 32)), -0.2, 0.2), 0.05, 0.95),
        "rates_newer": jnp.clip(0.05 + 0.9 * jax.random.uniform(key_list[3], (N_COL, N_ROW, GROUP, RUNS, STEPS), jnp.float32) ** block_scale(key_list[3], (N_COL, N_ROW, GROUP, RUNS, STEPS), ((0, 16), (1, 32)), -0.2, 0.2), 0.05, 0.95),
        "drive": gaussian(key_list[4], (SLABS, N_COL, N_ROW, GROUP, RUNS, STEPS), 1.0, 6.0, ((1, 16), (2, 32)), jnp.float32),
        "syn_kernel": draw_syn_kernel(jax.random.fold_in(key_list[6], 71), 0),
    }


PRECISE = lax.Precision.HIGHEST


def coupling_sum(coupling, lag_class, near_slab, far_slab):
    blocks = coupling.reshape(N_COL, N_ROW * GROUP, N_ROW, N_COL * GROUP)

    def one_source(row_index, total):
        index = jnp.asarray(row_index).astype(jnp.int32)
        weights = lax.dynamic_index_in_dim(blocks, index, 2, keepdims=False)
        near_rows = lax.dynamic_index_in_dim(near_slab, index, 1, keepdims=False).reshape(N_COL * GROUP, RUNS * STEPS)
        far_rows = lax.dynamic_index_in_dim(far_slab, index, 1, keepdims=False).reshape(N_COL * GROUP, RUNS * STEPS)
        lags = lax.dynamic_index_in_dim(lag_class, index, 1, keepdims=False)
        chosen = jnp.where((lags == 0)[:, None, None], near_rows[None], far_rows[None])
        return total + jnp.einsum("apq,aqs->aps", weights, chosen, precision=PRECISE)

    start = jnp.zeros((N_COL, N_ROW * GROUP, RUNS * STEPS), jnp.float32)
    total = lax.fori_loop(0, N_ROW, one_source, start)
    return total.reshape(N_COL, N_ROW, GROUP, RUNS, STEPS)


def reference(coupling, lag_class, rates_older, rates_newer, drive, syn_kernel):
    far_slab, near_slab = rates_older, rates_newer
    produced = []
    for slab_index in range(SLABS):
        inputs = coupling_sum(coupling, lag_class, near_slab, far_slab)
        filtered = jnp.einsum("abcrs,ts->abcrt", inputs, syn_kernel, precision=PRECISE)
        fresh = jax.nn.sigmoid(filtered + drive[slab_index])
        produced.append(fresh)
        far_slab, near_slab = near_slab, fresh
    return jnp.stack(produced)
```

```python
import functools

import jax
import jax.numpy as jnp
from jax import lax
from jax.experimental import pallas as pl
from jax.experimental.pallas import tpu as pltpu
from jax.sharding import PartitionSpec as P

MESH = pl.DeviceIdType.MESH
N_Z = 16
ROWS = 32
LANES = 128
SLABS = 3
RUNS = 2
LAG = 3

OFFSETS = (8, 7, -7, 6, 5, -6, -5, 4, 3, -4, -3, 2, 1, -2, -1, 0)
PLACE = {offset: place for place, offset in enumerate(OFFSETS)}
PLACE[-8] = PLACE[8]
GROUPS = ((0, 3), (3, 7), (7, 11), (11, 15), (15, 16))


def kernel(
    coupling, lag_class, older, newer, drive, syn_kernel, out,
    w_raw, w_hi, w_lo, seen, rhs, own, x_send, x_recv, z_send, z_recv, z_last,
    older_v, newer_v, drive_v, syn_v, kt_hi, kt_lo,
    load_sem, w_sem, gather_sem, x_sem, z_sem, last_sem, send_sem, first_send_sem,
):
    row, col = lax.axis_index("row"), lax.axis_index("col")
    z, x_lo = row // 2, row % 2
    x_hi, y, core = col // 8, (col // 2) % 4, col % 2

    loads = [
        pltpu.make_async_copy(src, dst, load_sem.at[i])
        for i, (src, dst) in enumerate(
            ((older, older_v), (newer, newer_v), (drive, drive_v), (syn_kernel, syn_v))
        )
    ]
    for load in loads:
        load.start()

    def z_device(step):
        return (lax.rem(z + step + N_Z, N_Z) * 2 + x_lo, col)

    x_device = (z * 2 + 1 - x_lo, col)
    peers = []
    for dx in (1, 0):
        for dy in (2, 1, 3, 0):
            for dc in (1, 0):
                if (dx, dy, dc) != (0, 0, 0):
                    other = (
                        lax.rem(x_hi + dx, 2) * 8
                        + lax.rem(y + dy, 4) * 2
                        + lax.rem(core + dc, 2)
                    )
                    peers.append((row, other))

    barrier = pltpu.get_barrier_semaphore()
    partners = peers + [x_device] + [z_device(s) for s in (1, -1, 2, -2)]
    for device in partners:
        pl.semaphore_signal(barrier, inc=1, device_id=device, device_id_type=MESH)

    w_loads = []
    for half in range(2):
        for place, offset in enumerate(OFFSETS):
            x_of = 1 - x_lo if half == 0 else x_lo
            block = lax.rem(z + offset + N_Z, N_Z) * 2 + x_of
            at = half * 16 + place
            w_loads.append(
                pltpu.make_async_copy(
                    coupling.at[pl.ds(pl.multiple_of(block * 128, 128), 128)],
                    w_raw.at[pl.ds(at * 128, 128)],
                    w_sem.at[at],
                )
            )
    for load in w_loads:
        load.start()

    mine = pl.multiple_of(col * ROWS, ROWS)

    def send_all(slab, run, sem, recv):
        block = seen.at[slab, run, pl.ds(mine, ROWS)]
        for device in peers:
            pltpu.make_async_remote_copy(
                src_ref=block, dst_ref=block, send_sem=sem, recv_sem=recv,
                device_id=device, device_id_type=MESH,
            ).start()

    loads[0].wait()
    loads[1].wait()
    for run in range(RUNS):
        seen[0, run, pl.ds(mine, ROWS), :] = older_v[pl.ds(run, ROWS, stride=2), :]
        seen[1, run, pl.ds(mine, ROWS), :] = newer_v[pl.ds(run, ROWS, stride=2), :]
    pl.semaphore_wait(barrier, len(partners))
    for run in range(RUNS):
        for slab in range(2):
            send_all(slab, run, first_send_sem.at[slab, run], gather_sem.at[slab, run])

    loads[2].wait()
    loads[3].wait()
    kt = syn_v[...].T
    kt_h = kt.astype(jnp.bfloat16)
    kt_hi[...] = kt_h
    kt_lo[...] = (kt - kt_h.astype(jnp.float32)).astype(jnp.bfloat16)

    for load in w_loads:
        load.wait()

    def split(at, carry):
        rows = pl.ds(pl.multiple_of(at * ROWS, ROWS), ROWS)
        for q in range(4):
            w = w_raw[pl.ds(at * 128 + q, ROWS, stride=4), :]
            w_h = w.astype(jnp.bfloat16)
            w_hi[rows, q * LANES : (q + 1) * LANES] = w_h
            w_lo[rows, q * LANES : (q + 1) * LANES] = (
                w - w_h.astype(jnp.float32)
            ).astype(jnp.bfloat16)
        return carry

    lax.fori_loop(0, 32, split, 0)

    def gather_wait(slab, run):
        rest = seen.at[slab, run, pl.ds(0, 15 * ROWS)]
        pltpu.make_async_copy(rest, rest, gather_sem.at[slab, run]).wait()

    def product(run, first, count):
        rows = pl.ds(first * ROWS, count * ROWS)
        both = jnp.dot(w_hi[rows, :], rhs[run], preferred_element_type=jnp.float32)
        low = jnp.dot(
            w_lo[rows, :], rhs[run, :, :LANES], preferred_element_type=jnp.float32
        )
        return both[:, :LANES] + (both[:, LANES:] + low)

    def x_copy(slab, run, group):
        first, last = GROUPS[group]
        rows = pl.ds(first * ROWS, (last - first) * ROWS)
        return pltpu.make_async_remote_copy(
            src_ref=x_send.at[slab, run, rows],
            dst_ref=x_recv.at[slab, run, rows],
            send_sem=send_sem.at[slab, run],
            recv_sem=x_sem.at[slab, run, group],
            device_id=x_device, device_id_type=MESH,
        )

    def multiply(slab, run):
        if slab == 0:
            gather_wait(0, run)
        gather_wait(slab + 1, run)
        lag = jnp.broadcast_to(lag_class[0, 0], (16 * ROWS, LANES))
        chosen = jnp.where(lag == 0, seen[slab + 1, run], seen[slab, run])
        high = chosen.astype(jnp.bfloat16)
        rhs[run, :, :LANES] = high
        rhs[run, :, LANES:] = (chosen - high.astype(jnp.float32)).astype(jnp.bfloat16)
        for group, (first, last) in enumerate(GROUPS):
            x_send[slab, run, first * ROWS : last * ROWS, :] = product(run, first, last - first)
            x_copy(slab, run, group).start()
        for first, last in GROUPS:
            own[slab, run, first * ROWS : last * ROWS, :] = product(
                run, 16 + first, last - first
            )

    def pair_offsets(way, run, step):
        sign = 1 if way == 0 else -1
        far, near = sign * (8 - 2 * step), sign * (7 - 2 * step)
        return (None if step == 0 and way != run else far), near

    def z_copy(slab, run, way, step):
        far, _ = pair_offsets(way, run, step)
        first = 0 if far is not None else ROWS
        rows = pl.ds(step * 2 * ROWS + first, 2 * ROWS - first)
        return pltpu.make_async_remote_copy(
            src_ref=z_send.at[slab, run, way, rows],
            dst_ref=z_recv.at[slab, run, way, rows],
            send_sem=send_sem.at[slab, run],
            recv_sem=z_sem.at[slab, run, way, step],
            device_id=z_device(2 if way == 0 else -2), device_id_type=MESH,
        )

    def last_copy(slab, run, way, which):
        sign = 1 if way == 0 else -1
        return pltpu.make_async_remote_copy(
            src_ref=z_send.at[slab, run, way, pl.ds((6 + which) * ROWS, ROWS)],
            dst_ref=z_last.at[slab, run, pl.ds((2 * way + which) * ROWS, ROWS)],
            send_sem=send_sem.at[slab, run],
            recv_sem=last_sem.at[slab, run, way, which],
            device_id=z_device(sign * (2 - which)), device_id_type=MESH,
        )

    def pass_on(slab, run, step):
        x_copy(slab, run, step).wait_recv()
        for way in range(2):
            if step:
                z_copy(slab, run, way, step - 1).wait_recv()
            for which, offset in enumerate(pair_offsets(way, run, step)):
                if offset is None:
                    continue
                at = PLACE[offset] * ROWS
                total = (
                    own[slab, run, at : at + ROWS, :] + x_recv[slab, run, at : at + ROWS, :]
                )
                if step and pair_offsets(way, run, step - 1)[which] is not None:
                    came = ((step - 1) * 2 + which) * ROWS
                    total = total + z_recv[slab, run, way, came : came + ROWS, :]
                to = (step * 2 + which) * ROWS
                z_send[slab, run, way, to : to + ROWS, :] = total
            if step < 3:
                z_copy(slab, run, way, step).start()
            else:
                for which in range(2):
                    last_copy(slab, run, way, which).start()

    def finish(slab, run):
        x_copy(slab, run, 4).wait_recv()
        total = own[slab, run, 15 * ROWS :, :] + x_recv[slab, run, 15 * ROWS :, :]
        for which in (1, 0):
            for way in range(2):
                last_copy(slab, run, way, which).wait_recv()
                came = (2 * way + which) * ROWS
                total = total + z_last[slab, run, came : came + ROWS, :]
        high = total.astype(jnp.bfloat16)
        low = (total - high.astype(jnp.float32)).astype(jnp.bfloat16)
        filtered = jnp.dot(high, kt_hi[...], preferred_element_type=jnp.float32) + (
            jnp.dot(high, kt_lo[...], preferred_element_type=jnp.float32)
            + jnp.dot(low, kt_hi[...], preferred_element_type=jnp.float32)
        )
        value = filtered + drive_v[slab, pl.ds(run, ROWS, stride=2), :]
        fresh = 1.0 / (1.0 + jnp.exp(-value))
        if slab < SLABS - 1:
            seen[slab + 2, run, pl.ds(mine, ROWS), :] = fresh
            send_all(slab + 2, run, send_sem.at[slab, run], gather_sem.at[slab + 2, run])
        out[slab, pl.ds(run, ROWS, stride=2), :] = fresh

    stages = []
    for run in range(RUNS):
        line = []
        for slab in range(SLABS):
            line.append(functools.partial(multiply, slab, run))
            for step in range(4):
                line.append(functools.partial(pass_on, slab, run, step))
            line.append(functools.partial(finish, slab, run))
        stages.append(line)
    for at in range(len(stages[0]) + LAG):
        for run in range(RUNS):
            if 0 <= at - LAG * run < len(stages[run]):
                stages[run][at - LAG * run]()

    for run in range(RUNS):
        for slab in range(2):
            rest = seen.at[slab, run, pl.ds(0, 15 * ROWS)]
            pltpu.make_async_copy(rest, rest, first_send_sem.at[slab, run]).wait()
        for slab in range(SLABS):
            blocks = 16 + 15 + (15 if slab < SLABS - 1 else 0)
            sent = w_raw.at[pl.ds(0, blocks * ROWS)]
            pltpu.make_async_copy(sent, sent, send_sem.at[slab, run]).wait()


def per_device(coupling, lag_class, rates_older, rates_newer, drive, syn_kernel):
    f32, bf16 = jnp.float32, jnp.bfloat16
    rates = pl.pallas_call(
        kernel,
        out_shape=jax.ShapeDtypeStruct((SLABS, 64, LANES), f32),
        in_specs=[
            pl.BlockSpec(memory_space=pl.ANY),
            pl.BlockSpec(memory_space=pltpu.SMEM),
            pl.BlockSpec(memory_space=pl.ANY),
            pl.BlockSpec(memory_space=pl.ANY),
            pl.BlockSpec(memory_space=pl.ANY),
            pl.BlockSpec(memory_space=pl.ANY),
        ],
        out_specs=pl.BlockSpec(memory_space=pltpu.VMEM),
        scratch_shapes=[
            pltpu.VMEM((4096, LANES), f32),
            pltpu.VMEM((1024, 512), bf16),
            pltpu.VMEM((1024, 512), bf16),
            pltpu.VMEM((4, RUNS, 512, LANES), f32),
            pltpu.VMEM((RUNS, 512, 2 * LANES), bf16),
            pltpu.VMEM((SLABS, RUNS, 512, LANES), f32),
            pltpu.VMEM((SLABS, RUNS, 512, LANES), f32),
            pltpu.VMEM((SLABS, RUNS, 512, LANES), f32),
            pltpu.VMEM((SLABS, RUNS, 2, 8 * ROWS, LANES), f32),
            pltpu.VMEM((SLABS, RUNS, 2, 8 * ROWS, LANES), f32),
            pltpu.VMEM((SLABS, RUNS, 4 * ROWS, LANES), f32),
            pltpu.VMEM((64, LANES), f32),
            pltpu.VMEM((64, LANES), f32),
            pltpu.VMEM((SLABS, 64, LANES), f32),
            pltpu.VMEM((LANES, LANES), f32),
            pltpu.VMEM((LANES, LANES), bf16),
            pltpu.VMEM((LANES, LANES), bf16),
            pltpu.SemaphoreType.DMA((4,)),
            pltpu.SemaphoreType.DMA((32,)),
            pltpu.SemaphoreType.DMA((4, RUNS)),
            pltpu.SemaphoreType.DMA((SLABS, RUNS, 5)),
            pltpu.SemaphoreType.DMA((SLABS, RUNS, 2, 3)),
            pltpu.SemaphoreType.DMA((SLABS, RUNS, 2, 2)),
            pltpu.SemaphoreType.DMA((SLABS, RUNS)),
            pltpu.SemaphoreType.DMA((2, RUNS)),
        ],
        compiler_params=pltpu.CompilerParams(collective_id=0, has_side_effects=True),
    )(
        coupling.reshape(4096, LANES),
        lag_class,
        rates_older.reshape(64, LANES),
        rates_newer.reshape(64, LANES),
        drive.reshape(SLABS, 64, LANES),
        syn_kernel,
    )
    return rates.reshape(drive.shape)


def solution(mesh):
    return jax.shard_map(
        per_device,
        mesh=mesh,
        in_specs=(
            P("col", "row", None),
            P("col", "row"),
            P("col", "row", None, None, None),
            P("col", "row", None, None, None),
            P(None, "col", "row", None, None, None),
            P(),
        ),
        out_specs=P(None, "col", "row", None, None, None),
        check_vma=False,
    )
```

```python
import functools

import jax
import jax.numpy as jnp
from jax import lax
from jax.experimental import pallas as pl
from jax.experimental.pallas import tpu as pltpu
from jax.sharding import PartitionSpec as P

MESH = pl.DeviceIdType.MESH
N_Z = 16
ROWS = 32
LANES = 128
SLABS = 3
RUNS = 2
LAG = 1
PIECE = 32

OFFSETS = (8, 7, -7, 6, 5, -6, -5, 4, 3, -4, -3, 2, 1, -2, -1, 0)
PLACE = {offset: place for place, offset in enumerate(OFFSETS)}
PLACE[-8] = PLACE[8]
PIECES = ROWS // PIECE
GROUPS = ((0, 3), (3, 7), (7, 11), (11, 15), (15, 16))


def kernel(
    coupling, lag_class, older, newer, drive, syn_kernel, out,
    w_raw, w_hi, w_lo, seen, rhs, own, x_send, x_recv, z_send, z_recv,
    older_v, newer_v, drive_v, syn_v, kt_hi, kt_lo,
    load_sem, w_sem, gather_sem, relay_sem, x_sem, z_sem, send_sem, first_send_sem,
):
    row, col = lax.axis_index("row"), lax.axis_index("col")
    z, x_lo = row // 2, row % 2
    x_hi, y, core = col // 8, (col // 2) % 4, col % 2

    loads = [
        pltpu.make_async_copy(src, dst, load_sem.at[i])
        for i, (src, dst) in enumerate(
            ((older, older_v), (newer, newer_v), (drive, drive_v), (syn_kernel, syn_v))
        )
    ]
    for load in loads:
        load.start()

    def z_device(step):
        return (lax.rem(z + step + N_Z, N_Z) * 2 + x_lo, col)

    x_device = (z * 2 + 1 - x_lo, col)
    peers = [
        (row, lax.rem(x_hi + dx, 2) * 8 + lax.rem(y + dy, 4) * 2 + core)
        for dx, dy in ((1, 2), (1, 1), (1, 3), (1, 0), (0, 2), (0, 1), (0, 3))
    ]
    sibling = (row, col + 1 - 2 * core)

    barrier = pltpu.get_barrier_semaphore()
    partners = peers + [sibling, x_device] + [z_device(s) for s in (1, -1, 2, -2)]
    for device in partners:
        pl.semaphore_signal(barrier, inc=1, device_id=device, device_id_type=MESH)

    w_loads = []
    for half in range(2):
        for place, offset in enumerate(OFFSETS):
            x_of = 1 - x_lo if half == 0 else x_lo
            block = lax.rem(z + offset + N_Z, N_Z) * 2 + x_of
            at = half * 16 + place
            w_loads.append(
                pltpu.make_async_copy(
                    coupling.at[pl.ds(pl.multiple_of(block * 128, 128), 128)],
                    w_raw.at[pl.ds(at * 128, 128)],
                    w_sem.at[at],
                )
            )
    for load in w_loads:
        load.start()

    chip = x_hi * 4 + y

    def send_all(slab, run, sem, recv):
        block = seen.at[slab, run, chip, core]
        for device in peers:
            pltpu.make_async_remote_copy(
                src_ref=block, dst_ref=block, send_sem=sem, recv_sem=recv,
                device_id=device, device_id_type=MESH,
            ).start()

    loads[0].wait()
    loads[1].wait()
    for run in range(RUNS):
        seen[0, run, chip, core] = older_v[pl.ds(run, ROWS, stride=2), :]
        seen[1, run, chip, core] = newer_v[pl.ds(run, ROWS, stride=2), :]
    pl.semaphore_wait(barrier, len(partners))
    for run in range(RUNS):
        for slab in (1, 0):
            send_all(slab, run, first_send_sem.at[slab, run], gather_sem.at[slab, run])

    loads[2].wait()
    loads[3].wait()
    kt = syn_v[...].T
    kt_h = kt.astype(jnp.bfloat16)
    kt_hi[...] = kt_h
    kt_lo[...] = (kt - kt_h.astype(jnp.float32)).astype(jnp.bfloat16)

    for load in w_loads:
        load.wait()

    def split(at, carry):
        rows = pl.ds(pl.multiple_of(at * ROWS, ROWS), ROWS)
        for q in range(4):
            w = w_raw[pl.ds(at * 128 + q, ROWS, stride=4), :]
            w_h = w.astype(jnp.bfloat16)
            w_hi[rows, q * LANES : (q + 1) * LANES] = w_h
            w_lo[rows, q * LANES : (q + 1) * LANES] = (
                w - w_h.astype(jnp.float32)
            ).astype(jnp.bfloat16)
        return carry

    lax.fori_loop(0, 32, split, 0)

    def relay_copy(slab, run):
        blocks = seen.at[slab, run, :, core]
        sem = first_send_sem.at[slab, run] if slab < 2 else send_sem.at[slab - 2, run]
        return pltpu.make_async_remote_copy(
            src_ref=blocks, dst_ref=blocks, send_sem=sem, recv_sem=relay_sem.at[slab, run],
            device_id=sibling, device_id_type=MESH,
        )

    def relay(slab, run):
        for of in (1, 0) if slab == 0 else (slab + 1,):
            rest = seen.at[of, run, pl.ds(0, 7), 0]
            pltpu.make_async_copy(rest, rest, gather_sem.at[of, run]).wait()
            relay_copy(of, run).start()

    def product(run, first, count):
        rows = pl.ds(first * ROWS, count * ROWS)
        both = jnp.dot(w_hi[rows, :], rhs[run], preferred_element_type=jnp.float32)
        low = jnp.dot(
            w_lo[rows, :], rhs[run, :, :LANES], preferred_element_type=jnp.float32
        )
        return both[:, :LANES] + (both[:, LANES:] + low)

    def x_copy(slab, run, group):
        first, last = GROUPS[group]
        rows = pl.ds(first * ROWS, (last - first) * ROWS)
        return pltpu.make_async_remote_copy(
            src_ref=x_send.at[slab, run, rows],
            dst_ref=x_recv.at[slab, run, rows],
            send_sem=send_sem.at[slab, run],
            recv_sem=x_sem.at[slab, run, group],
            device_id=x_device, device_id_type=MESH,
        )

    def multiply(slab, run):
        if slab == 0:
            relay_copy(0, run).wait_recv()
        relay_copy(slab + 1, run).wait_recv()
        lag = jnp.broadcast_to(lag_class[0, 0], (16 * ROWS, LANES))
        near = seen[slab + 1, run].reshape(16 * ROWS, LANES)
        far = seen[slab, run].reshape(16 * ROWS, LANES)
        chosen = jnp.where(lag == 0, near, far)
        high = chosen.astype(jnp.bfloat16)
        rhs[run, :, :LANES] = high
        rhs[run, :, LANES:] = (chosen - high.astype(jnp.float32)).astype(jnp.bfloat16)
        for group, (first, last) in enumerate(GROUPS):
            x_send[slab, run, first * ROWS : last * ROWS, :] = product(run, first, last - first)
            x_copy(slab, run, group).start()
        for first, last in GROUPS:
            own[slab, run, first * ROWS : last * ROWS, :] = product(
                run, 16 + first, last - first
            )

    def pair_offsets(way, run, step):
        sign = 1 if way == 0 else -1
        far, near = sign * (8 - 2 * step), sign * (7 - 2 * step)
        return (None if step == 0 and way != run else far), near

    def z_copy(slab, run, way, step, which, piece):
        sign = 1 if way == 0 else -1
        rows = pl.ds((step * 2 + which) * ROWS + piece * PIECE, PIECE)
        at = ((step * 2 + which) * 2 + way) * PIECES + piece
        return pltpu.make_async_remote_copy(
            src_ref=z_send.at[slab, run, way, rows],
            dst_ref=z_recv.at[slab, run, way, rows],
            send_sem=send_sem.at[slab, run],
            recv_sem=z_sem.at[slab, run, at],
            device_id=z_device(sign * (1 if step == 3 and which == 1 else 2)),
            device_id_type=MESH,
        )

    def pass_on(slab, run, step):
        x_copy(slab, run, step).wait_recv()
        for which in range(2):
            for piece in range(PIECES):
                for way in range(2):
                    offset = pair_offsets(way, run, step)[which]
                    if offset is None:
                        continue
                    at = PLACE[offset] * ROWS + piece * PIECE
                    total = (
                        own[slab, run, at : at + PIECE, :]
                        + x_recv[slab, run, at : at + PIECE, :]
                    )
                    if step and pair_offsets(way, run, step - 1)[which] is not None:
                        z_copy(slab, run, way, step - 1, which, piece).wait_recv()
                        came = ((step - 1) * 2 + which) * ROWS + piece * PIECE
                        total = total + z_recv[slab, run, way, came : came + PIECE, :]
                    to = (step * 2 + which) * ROWS + piece * PIECE
                    z_send[slab, run, way, to : to + PIECE, :] = total
                    z_copy(slab, run, way, step, which, piece).start()

    def finish(slab, run):
        x_copy(slab, run, 4).wait_recv()
        total = own[slab, run, 15 * ROWS :, :] + x_recv[slab, run, 15 * ROWS :, :]
        for which in range(2):
            for way in range(2):
                for piece in range(PIECES):
                    z_copy(slab, run, way, 3, which, piece).wait_recv()
                came = (6 + which) * ROWS
                total = total + z_recv[slab, run, way, came : came + ROWS, :]
        high = total.astype(jnp.bfloat16)
        low = (total - high.astype(jnp.float32)).astype(jnp.bfloat16)
        filtered = jnp.dot(high, kt_hi[...], preferred_element_type=jnp.float32) + (
            jnp.dot(high, kt_lo[...], preferred_element_type=jnp.float32)
            + jnp.dot(low, kt_hi[...], preferred_element_type=jnp.float32)
        )
        value = filtered + drive_v[slab, pl.ds(run, ROWS, stride=2), :]
        fresh = 1.0 / (1.0 + jnp.exp(-value))
        if slab < SLABS - 1:
            seen[slab + 2, run, chip, core] = fresh
            send_all(slab + 2, run, send_sem.at[slab, run], gather_sem.at[slab + 2, run])
        out[slab, pl.ds(run, ROWS, stride=2), :] = fresh

    stages = []
    for run in range(RUNS):
        line = []
        for slab in range(SLABS):
            line.append(functools.partial(relay, slab, run))
            line.append(functools.partial(multiply, slab, run))
            for step in range(4):
                line.append(functools.partial(pass_on, slab, run, step))
            line.append(functools.partial(finish, slab, run))
        stages.append(line)
    for at in range(len(stages[0]) + LAG):
        for run in range(RUNS):
            if 0 <= at - LAG * run < len(stages[run]):
                stages[run][at - LAG * run]()

    for run in range(RUNS):
        for slab in range(2):
            sent = w_raw.at[pl.ds(0, 15 * ROWS)]
            pltpu.make_async_copy(sent, sent, first_send_sem.at[slab, run]).wait()
        for slab in range(SLABS):
            blocks = 16 + 15 + (15 if slab < SLABS - 1 else 0)
            sent = w_raw.at[pl.ds(0, blocks * ROWS)]
            pltpu.make_async_copy(sent, sent, send_sem.at[slab, run]).wait()


def per_device(coupling, lag_class, rates_older, rates_newer, drive, syn_kernel):
    f32, bf16 = jnp.float32, jnp.bfloat16
    rates = pl.pallas_call(
        kernel,
        out_shape=jax.ShapeDtypeStruct((SLABS, 64, LANES), f32),
        in_specs=[
            pl.BlockSpec(memory_space=pl.ANY),
            pl.BlockSpec(memory_space=pltpu.SMEM),
            pl.BlockSpec(memory_space=pl.ANY),
            pl.BlockSpec(memory_space=pl.ANY),
            pl.BlockSpec(memory_space=pl.ANY),
            pl.BlockSpec(memory_space=pl.ANY),
        ],
        out_specs=pl.BlockSpec(memory_space=pltpu.VMEM),
        scratch_shapes=[
            pltpu.VMEM((4096, LANES), f32),
            pltpu.VMEM((1024, 512), bf16),
            pltpu.VMEM((1024, 512), bf16),
            pltpu.VMEM((4, RUNS, 8, 2, ROWS, LANES), f32),
            pltpu.VMEM((RUNS, 512, 2 * LANES), bf16),
            pltpu.VMEM((SLABS, RUNS, 512, LANES), f32),
            pltpu.VMEM((SLABS, RUNS, 512, LANES), f32),
            pltpu.VMEM((SLABS, RUNS, 512, LANES), f32),
            pltpu.VMEM((SLABS, RUNS, 2, 8 * ROWS, LANES), f32),
            pltpu.VMEM((SLABS, RUNS, 2, 8 * ROWS, LANES), f32),
            pltpu.VMEM((64, LANES), f32),
            pltpu.VMEM((64, LANES), f32),
            pltpu.VMEM((SLABS, 64, LANES), f32),
            pltpu.VMEM((LANES, LANES), f32),
            pltpu.VMEM((LANES, LANES), bf16),
            pltpu.VMEM((LANES, LANES), bf16),
            pltpu.SemaphoreType.DMA((4,)),
            pltpu.SemaphoreType.DMA((32,)),
            pltpu.SemaphoreType.DMA((4, RUNS)),
            pltpu.SemaphoreType.DMA((4, RUNS)),
            pltpu.SemaphoreType.DMA((SLABS, RUNS, 5)),
            pltpu.SemaphoreType.DMA((SLABS, RUNS, 16 * PIECES)),
            pltpu.SemaphoreType.DMA((SLABS, RUNS)),
            pltpu.SemaphoreType.DMA((2, RUNS)),
        ],
        compiler_params=pltpu.CompilerParams(collective_id=0, has_side_effects=True),
    )(
        coupling.reshape(4096, LANES),
        lag_class,
        rates_older.reshape(64, LANES),
        rates_newer.reshape(64, LANES),
        drive.reshape(SLABS, 64, LANES),
        syn_kernel,
    )
    return rates.reshape(drive.shape)


def solution(mesh):
    return jax.shard_map(
        per_device,
        mesh=mesh,
        in_specs=(
            P("col", "row", None),
            P("col", "row"),
            P("col", "row", None, None, None),
            P("col", "row", None, None, None),
            P(None, "col", "row", None, None, None),
            P(),
        ),
        out_specs=P(None, "col", "row", None, None, None),
        check_vma=False,
    )
```

```python
import functools

import jax
import jax.numpy as jnp
from jax import lax
from jax.experimental import pallas as pl
from jax.experimental.pallas import tpu as pltpu
from jax.sharding import PartitionSpec as P

MESH = pl.DeviceIdType.MESH
N_Z = 16
ROWS = 32
LANES = 128
SLABS = 3
RUNS = 2
TAU = 4.0
STAGE_US = (5.3, 6.5, 9.9, 12.6, 15.3, 18.0)
SLAB_US = 19.5
PIECE = 32
AHEAD = 3

OFFSETS = (8, 7, -7, 6, 5, -6, -5, 4, 3, -4, -3, 2, 1, -2, -1, 0)
PLACE = {offset: place for place, offset in enumerate(OFFSETS)}
PLACE[-8] = PLACE[8]
PIECES = ROWS // PIECE
GROUPS = ((0, 3), (3, 7), (7, 11), (11, 15), (15, 16))


def kernel(
    coupling, lag_class, older, newer, drive, syn_kernel, out,
    w_raw, w_hi, w_lo, seen, rhs, own, x_send, x_recv, z_send, z_recv, d_recv,
    older_v, newer_v, drive_v, syn_v, lag_v, kt_hi, kt_lo,
    load_sem, w_sem, gather_sem, relay_sem, x_sem, z_sem, d_sem, send_sem, first_send_sem,
):
    row, col = lax.axis_index("row"), lax.axis_index("col")
    z, x_lo = row // 2, row % 2
    x_hi, y, core = col // 8, (col // 2) % 4, col % 2

    loads = [
        pltpu.make_async_copy(src, dst, load_sem.at[i])
        for i, (src, dst) in enumerate(
            ((older, older_v), (newer, newer_v), (drive, drive_v), (syn_kernel, syn_v),
             (lag_class, lag_v))
        )
    ]
    for load in loads:
        load.start()

    def z_device(step, across=False):
        x_of = 1 - x_lo if across else x_lo
        return (lax.rem(z + step + N_Z, N_Z) * 2 + x_of, col)

    x_device = (z * 2 + 1 - x_lo, col)
    peers = [
        (row, lax.rem(x_hi + dx, 2) * 8 + lax.rem(y + dy, 4) * 2 + core)
        for dx, dy in ((1, 2), (1, 1), (1, 3), (1, 0), (0, 2), (0, 1), (0, 3))
    ]
    sibling = (row, col + 1 - 2 * core)

    barrier = pltpu.get_barrier_semaphore()
    partners = peers + [sibling, x_device] + [z_device(s) for s in (1, -1, 2, -2)]
    partners += [z_device(2, True), z_device(-2, True)]
    for device in partners:
        pl.semaphore_signal(barrier, inc=1, device_id=device, device_id_type=MESH)

    w_loads = []
    for half in range(2):
        for place, offset in enumerate(OFFSETS):
            x_of = 1 - x_lo if half == 0 else x_lo
            block = lax.rem(z + offset + N_Z, N_Z) * 2 + x_of
            at = half * 16 + place
            w_loads.append(
                pltpu.make_async_copy(
                    coupling.at[pl.ds(pl.multiple_of(block * 128, 128), 128)],
                    w_raw.at[pl.ds(at * 128, 128)],
                    w_sem.at[at],
                )
            )
    for load in w_loads:
        load.start()

    chip = x_hi * 4 + y

    def send_all(slab, run, sem, recv):
        block = seen.at[slab, run, chip, core]
        for device in peers:
            pltpu.make_async_remote_copy(
                src_ref=block, dst_ref=block, send_sem=sem, recv_sem=recv,
                device_id=device, device_id_type=MESH,
            ).start()

    loads[0].wait()
    loads[1].wait()
    for run in range(RUNS):
        seen[0, run, chip, core] = older_v[pl.ds(run, ROWS, stride=2), :]
        seen[1, run, chip, core] = newer_v[pl.ds(run, ROWS, stride=2), :]
    pl.semaphore_wait(barrier, len(partners))
    for run in range(RUNS):
        for slab in (1, 0):
            send_all(slab, run, first_send_sem.at[slab, run], gather_sem.at[slab, run])

    loads[2].wait()
    loads[3].wait()
    loads[4].wait()
    kt = syn_v[...].T
    kt_h = kt.astype(jnp.bfloat16)
    kt_hi[...] = kt_h
    kt_lo[...] = (kt - kt_h.astype(jnp.float32)).astype(jnp.bfloat16)

    for load in w_loads:
        load.wait()

    def split(at, carry):
        rows = pl.ds(pl.multiple_of(at * ROWS, ROWS), ROWS)
        for q in range(4):
            w = w_raw[pl.ds(at * 128 + q, ROWS, stride=4), :]
            w_h = w.astype(jnp.bfloat16)
            w_hi[rows, q * LANES : (q + 1) * LANES] = w_h
            w_lo[rows, q * LANES : (q + 1) * LANES] = (
                w - w_h.astype(jnp.float32)
            ).astype(jnp.bfloat16)
        return carry

    lax.fori_loop(0, 32, split, 0)

    def relay_copy(slab, run):
        blocks = seen.at[slab, run, :, core]
        sem = first_send_sem.at[slab, run] if slab < 2 else send_sem.at[slab - 2, run]
        return pltpu.make_async_remote_copy(
            src_ref=blocks, dst_ref=blocks, send_sem=sem, recv_sem=relay_sem.at[slab, run],
            device_id=sibling, device_id_type=MESH,
        )

    def relay(slab, run):
        for of in (1, 0) if slab == 0 else (slab + 1,):
            rest = seen.at[of, run, pl.ds(0, 7), 0]
            pltpu.make_async_copy(rest, rest, gather_sem.at[of, run]).wait()
            relay_copy(of, run).start()

    def product(run, first, count):
        rows = pl.ds(first * ROWS, count * ROWS)
        both = jnp.dot(w_hi[rows, :], rhs[run], preferred_element_type=jnp.float32)
        low = jnp.dot(
            w_lo[rows, :], rhs[run, :, :LANES], preferred_element_type=jnp.float32
        )
        return both[:, :LANES] + (both[:, LANES:] + low)

    def x_copy(slab, run, group):
        first, last = GROUPS[group]
        rows = pl.ds(first * ROWS, (last - first) * ROWS)
        return pltpu.make_async_remote_copy(
            src_ref=x_send.at[slab, run, rows],
            dst_ref=x_recv.at[slab, run, rows],
            send_sem=send_sem.at[slab, run],
            recv_sem=x_sem.at[slab, run, group],
            device_id=x_device, device_id_type=MESH,
        )

    def multiply(slab, run):
        if slab == 0:
            relay_copy(0, run).wait_recv()
        relay_copy(slab + 1, run).wait_recv()
        lag = jnp.broadcast_to(lag_v[...], (16 * ROWS, LANES))
        near = seen[slab + 1, run].reshape(16 * ROWS, LANES)
        far = seen[slab, run].reshape(16 * ROWS, LANES)
        chosen = jnp.where(lag == 0, near, far)
        high = chosen.astype(jnp.bfloat16)
        rhs[run, :, :LANES] = high
        rhs[run, :, LANES:] = (chosen - high.astype(jnp.float32)).astype(jnp.bfloat16)
        give(slab, run, 0)
        keep(slab, run, 0)
        pass_on(slab, run, 0)
        for group in range(1, AHEAD):
            give(slab, run, group)
        keep(slab, run, 1)

    def give(slab, run, group):
        first, last = GROUPS[group]
        x_send[slab, run, first * ROWS : last * ROWS, :] = product(run, first, last - first)
        if group:
            x_copy(slab, run, group).start()
            return
        for which in (0, 1):
            for way in range(2):
                if pair_offsets(way, run, 0)[which] is not None:
                    d_copy(slab, run, way, which).start()

    def keep(slab, run, group):
        first, last = GROUPS[group]
        own[slab, run, first * ROWS : last * ROWS, :] = product(run, 16 + first, last - first)

    def pair_offsets(way, run, step):
        sign = 1 if way == 0 else -1
        far, near = sign * (8 - 2 * step), sign * (7 - 2 * step)
        return (None if step == 0 and way != run else far), near

    def z_copy(slab, run, way, step, which, piece):
        sign = 1 if way == 0 else -1
        rows = pl.ds((step * 2 + which) * ROWS + piece * PIECE, PIECE)
        at = ((step * 2 + which) * 2 + way) * PIECES + piece
        return pltpu.make_async_remote_copy(
            src_ref=z_send.at[slab, run, way, rows],
            dst_ref=z_recv.at[slab, run, way, rows],
            send_sem=send_sem.at[slab, run],
            recv_sem=z_sem.at[slab, run, at],
            device_id=z_device(sign * (1 if step == 3 and which == 1 else 2)),
            device_id_type=MESH,
        )

    def d_copy(slab, run, way, which):
        at = PLACE[pair_offsets(way, run, 0)[which]] * ROWS
        return pltpu.make_async_remote_copy(
            src_ref=x_send.at[slab, run, pl.ds(at, ROWS)],
            dst_ref=d_recv.at[slab, run, pl.ds((way * 2 + which) * ROWS, ROWS)],
            send_sem=send_sem.at[slab, run],
            recv_sem=d_sem.at[slab, run, way * 2 + which],
            device_id=z_device(2 if way == 0 else -2, True), device_id_type=MESH,
        )

    def pass_on(slab, run, step):
        if step:
            x_copy(slab, run, step).wait_recv()
        for which in range(2):
            for piece in range(PIECES):
                for way in range(2):
                    offset = pair_offsets(way, run, step)[which]
                    if offset is None:
                        continue
                    at = PLACE[offset] * ROWS + piece * PIECE
                    total = own[slab, run, at : at + PIECE, :]
                    if step:
                        total = total + x_recv[slab, run, at : at + PIECE, :]
                    if step and pair_offsets(way, run, step - 1)[which] is not None:
                        z_copy(slab, run, way, step - 1, which, piece).wait_recv()
                        came = ((step - 1) * 2 + which) * ROWS + piece * PIECE
                        total = total + z_recv[slab, run, way, came : came + PIECE, :]
                        if step == 1:
                            d_copy(slab, run, way, which).wait_recv()
                            came = (way * 2 + which) * ROWS + piece * PIECE
                            total = total + d_recv[slab, run, came : came + PIECE, :]
                    to = (step * 2 + which) * ROWS + piece * PIECE
                    z_send[slab, run, way, to : to + PIECE, :] = total
                    z_copy(slab, run, way, step, which, piece).start()
        if step:
            if step + AHEAD - 1 < 5:
                give(slab, run, step + AHEAD - 1)
            keep(slab, run, step + 1)

    def finish(slab, run):
        x_copy(slab, run, 4).wait_recv()
        total = own[slab, run, 15 * ROWS :, :] + x_recv[slab, run, 15 * ROWS :, :]
        for which in range(2):
            for way in range(2):
                for piece in range(PIECES):
                    z_copy(slab, run, way, 3, which, piece).wait_recv()
                came = (6 + which) * ROWS
                total = total + z_recv[slab, run, way, came : came + ROWS, :]
        high = total.astype(jnp.bfloat16)
        low = (total - high.astype(jnp.float32)).astype(jnp.bfloat16)
        filtered = jnp.dot(high, kt_hi[...], preferred_element_type=jnp.float32) + (
            jnp.dot(high, kt_lo[...], preferred_element_type=jnp.float32)
            + jnp.dot(low, kt_hi[...], preferred_element_type=jnp.float32)
        )
        value = filtered + drive_v[slab, pl.ds(run, ROWS, stride=2), :]
        fresh = 1.0 / (1.0 + jnp.exp(-value))
        if slab < SLABS - 1:
            seen[slab + 2, run, chip, core] = fresh
            send_all(slab + 2, run, send_sem.at[slab, run], gather_sem.at[slab + 2, run])
        out[slab, pl.ds(run, ROWS, stride=2), :] = fresh

    stages = []
    for run in range(RUNS):
        line = []
        for slab in range(SLABS):
            line.append(functools.partial(relay, slab, run))
            line.append(functools.partial(multiply, slab, run))
            for step in range(1, 4):
                line.append(functools.partial(pass_on, slab, run, step))
            line.append(functools.partial(finish, slab, run))
        stages.append(line)
    order = []
    for run in range(RUNS):
        for at, stage in enumerate(stages[run]):
            due = at // 6 * SLAB_US + STAGE_US[at % 6] + run * TAU
            order.append((due, run, at, stage))
    for _, _, _, stage in sorted(order, key=lambda entry: entry[:3]):
        stage()

    for run in range(RUNS):
        for slab in range(2):
            sent = w_raw.at[pl.ds(0, 15 * ROWS)]
            pltpu.make_async_copy(sent, sent, first_send_sem.at[slab, run]).wait()
        for slab in range(SLABS):
            blocks = 16 + 15 + (15 if slab < SLABS - 1 else 0)
            sent = w_raw.at[pl.ds(0, blocks * ROWS)]
            pltpu.make_async_copy(sent, sent, send_sem.at[slab, run]).wait()


def per_device(coupling, lag_class, rates_older, rates_newer, drive, syn_kernel):
    f32, bf16 = jnp.float32, jnp.bfloat16
    rates = pl.pallas_call(
        kernel,
        out_shape=pltpu.VMEM((SLABS, 64, LANES), f32),
        in_specs=[
            pl.BlockSpec(memory_space=pl.ANY),
            pl.BlockSpec(memory_space=pl.ANY),
            pl.BlockSpec(memory_space=pl.ANY),
            pl.BlockSpec(memory_space=pl.ANY),
            pl.BlockSpec(memory_space=pl.ANY),
            pl.BlockSpec(memory_space=pl.ANY),
        ],
        out_specs=pl.BlockSpec(memory_space=pltpu.VMEM),
        scratch_shapes=[
            pltpu.VMEM((4096, LANES), f32),
            pltpu.VMEM((1024, 512), bf16),
            pltpu.VMEM((1024, 512), bf16),
            pltpu.VMEM((4, RUNS, 8, 2, ROWS, LANES), f32),
            pltpu.VMEM((RUNS, 512, 2 * LANES), bf16),
            pltpu.VMEM((SLABS, RUNS, 512, LANES), f32),
            pltpu.VMEM((SLABS, RUNS, 512, LANES), f32),
            pltpu.VMEM((SLABS, RUNS, 512, LANES), f32),
            pltpu.VMEM((SLABS, RUNS, 2, 8 * ROWS, LANES), f32),
            pltpu.VMEM((SLABS, RUNS, 2, 8 * ROWS, LANES), f32),
            pltpu.VMEM((SLABS, RUNS, 4 * ROWS, LANES), f32),
            pltpu.VMEM((64, LANES), f32),
            pltpu.VMEM((64, LANES), f32),
            pltpu.VMEM((SLABS, 64, LANES), f32),
            pltpu.VMEM((LANES, LANES), f32),
            pltpu.VMEM((1, 1), jnp.int32),
            pltpu.VMEM((LANES, LANES), bf16),
            pltpu.VMEM((LANES, LANES), bf16),
            pltpu.SemaphoreType.DMA((5,)),
            pltpu.SemaphoreType.DMA((32,)),
            pltpu.SemaphoreType.DMA((4, RUNS)),
            pltpu.SemaphoreType.DMA((4, RUNS)),
            pltpu.SemaphoreType.DMA((SLABS, RUNS, 5)),
            pltpu.SemaphoreType.DMA((SLABS, RUNS, 16 * PIECES)),
            pltpu.SemaphoreType.DMA((SLABS, RUNS, 4)),
            pltpu.SemaphoreType.DMA((SLABS, RUNS)),
            pltpu.SemaphoreType.DMA((2, RUNS)),
        ],
        compiler_params=pltpu.CompilerParams(collective_id=0, has_side_effects=True),
    )(
        coupling.reshape(4096, LANES),
        lag_class,
        rates_older.reshape(64, LANES),
        rates_newer.reshape(64, LANES),
        drive.reshape(SLABS, 64, LANES),
        syn_kernel,
    )
    return rates.reshape(drive.shape)


def solution(mesh):
    return jax.shard_map(
        per_device,
        mesh=mesh,
        in_specs=(
            P("col", "row", None),
            P("col", "row"),
            P("col", "row", None, None, None),
            P("col", "row", None, None, None),
            P(None, "col", "row", None, None, None),
            P(),
        ),
        out_specs=P(None, "col", "row", None, None, None),
        check_vma=False,
    )
```

```python
import functools

import jax
import jax.numpy as jnp
from jax import lax
from jax.experimental import pallas as pl
from jax.experimental.pallas import tpu as pltpu
from jax.sharding import PartitionSpec as P

MESH = pl.DeviceIdType.MESH
N_Z = 16
ROWS = 32
LANES = 128
SLABS = 3
RUNS = 2
TAU = 3.0
STAGE_US = (5.3, 6.5, 9.9, 12.6, 15.3, 18.0)
SLAB_US = 19.5
PIECE = 32
AHEAD = 3

OFFSETS = (8, 7, -7, 6, 5, -6, -5, 4, 3, -4, -3, 2, 1, -2, -1, 0)
PLACE = {offset: place for place, offset in enumerate(OFFSETS)}
PLACE[-8] = PLACE[8]
PIECES = ROWS // PIECE
GROUPS = ((0, 3), (3, 7), (7, 11), (11, 15), (15, 16))


def kernel(
    coupling, lag_class, older, newer, drive, syn_kernel, out,
    w_raw, w_hi, w_lo, seen, rhs, own, x_send, x_recv, z_send, z_recv, d_recv,
    older_v, newer_v, drive_v, syn_v, lag_v, kt_hi, kt_lo,
    load_sem, w_sem, gather_sem, relay_sem, x_sem, z_sem, d_sem, send_sem, first_send_sem,
):
    row, col = lax.axis_index("row"), lax.axis_index("col")
    z, x_lo = row // 2, row % 2
    x_hi, y, core = col // 8, (col // 2) % 4, col % 2

    loads = [
        pltpu.make_async_copy(src, dst, load_sem.at[i])
        for i, (src, dst) in enumerate(
            ((older, older_v), (newer, newer_v), (drive, drive_v), (syn_kernel, syn_v),
             (lag_class, lag_v))
        )
    ]
    for load in loads:
        load.start()

    def z_device(step, across=False):
        x_of = 1 - x_lo if across else x_lo
        return (lax.rem(z + step + N_Z, N_Z) * 2 + x_of, col)

    x_device = (z * 2 + 1 - x_lo, col)
    peers = [
        (row, lax.rem(x_hi + dx, 2) * 8 + lax.rem(y + dy, 4) * 2 + core)
        for dx, dy in ((1, 2), (1, 1), (1, 3), (1, 0), (0, 2), (0, 1), (0, 3))
    ]
    sibling = (row, col + 1 - 2 * core)

    barrier = pltpu.get_barrier_semaphore()
    partners = peers + [sibling, x_device] + [z_device(s) for s in (1, -1, 2, -2)]
    partners += [z_device(s, True) for s in (1, -1, 2, -2)]
    for device in partners:
        pl.semaphore_signal(barrier, inc=1, device_id=device, device_id_type=MESH)

    w_loads = []
    for half in range(2):
        for place, offset in enumerate(OFFSETS):
            x_of = 1 - x_lo if half == 0 else x_lo
            block = lax.rem(z + offset + N_Z, N_Z) * 2 + x_of
            at = half * 16 + place
            w_loads.append(
                pltpu.make_async_copy(
                    coupling.at[pl.ds(pl.multiple_of(block * 128, 128), 128)],
                    w_raw.at[pl.ds(at * 128, 128)],
                    w_sem.at[at],
                )
            )
    for load in w_loads:
        load.start()

    chip = x_hi * 4 + y

    def send_all(slab, run, sem, recv):
        block = seen.at[slab, run, chip, core]
        for device in peers:
            pltpu.make_async_remote_copy(
                src_ref=block, dst_ref=block, send_sem=sem, recv_sem=recv,
                device_id=device, device_id_type=MESH,
            ).start()

    loads[0].wait()
    loads[1].wait()
    for run in range(RUNS):
        seen[0, run, chip, core] = older_v[pl.ds(run, ROWS, stride=2), :]
        seen[1, run, chip, core] = newer_v[pl.ds(run, ROWS, stride=2), :]
    pl.semaphore_wait(barrier, len(partners))
    for run in range(RUNS):
        for slab in (1, 0):
            send_all(slab, run, first_send_sem.at[slab, run], gather_sem.at[slab, run])

    loads[2].wait()
    loads[3].wait()
    loads[4].wait()
    kt = syn_v[...].T
    kt_h = kt.astype(jnp.bfloat16)
    kt_hi[...] = kt_h
    kt_lo[...] = (kt - kt_h.astype(jnp.float32)).astype(jnp.bfloat16)

    for load in w_loads:
        load.wait()

    def split(at, carry):
        rows = pl.ds(pl.multiple_of(at * ROWS, ROWS), ROWS)
        for q in range(4):
            w = w_raw[pl.ds(at * 128 + q, ROWS, stride=4), :]
            w_h = w.astype(jnp.bfloat16)
            w_hi[rows, q * LANES : (q + 1) * LANES] = w_h
            w_lo[rows, q * LANES : (q + 1) * LANES] = (
                w - w_h.astype(jnp.float32)
            ).astype(jnp.bfloat16)
        return carry

    lax.fori_loop(0, 32, split, 0)

    def relay_copy(slab, run):
        blocks = seen.at[slab, run, :, core]
        sem = first_send_sem.at[slab, run] if slab < 2 else send_sem.at[slab - 2, run]
        return pltpu.make_async_remote_copy(
            src_ref=blocks, dst_ref=blocks, send_sem=sem, recv_sem=relay_sem.at[slab, run],
            device_id=sibling, device_id_type=MESH,
        )

    def relay(slab, run):
        for of in (1, 0) if slab == 0 else (slab + 1,):
            rest = seen.at[of, run, pl.ds(0, 7), 0]
            pltpu.make_async_copy(rest, rest, gather_sem.at[of, run]).wait()
            relay_copy(of, run).start()

    def product(run, first, count):
        rows = pl.ds(first * ROWS, count * ROWS)
        both = jnp.dot(w_hi[rows, :], rhs[run], preferred_element_type=jnp.float32)
        low = jnp.dot(
            w_lo[rows, :], rhs[run, :, :LANES], preferred_element_type=jnp.float32
        )
        return both[:, :LANES] + (both[:, LANES:] + low)

    def x_copy(slab, run, group):
        first, last = GROUPS[group]
        rows = pl.ds(first * ROWS, (last - first) * ROWS)
        return pltpu.make_async_remote_copy(
            src_ref=x_send.at[slab, run, rows],
            dst_ref=x_recv.at[slab, run, rows],
            send_sem=send_sem.at[slab, run],
            recv_sem=x_sem.at[slab, run, group],
            device_id=x_device, device_id_type=MESH,
        )

    def multiply(slab, run):
        if slab == 0:
            relay_copy(0, run).wait_recv()
        relay_copy(slab + 1, run).wait_recv()
        lag = jnp.broadcast_to(lag_v[...], (16 * ROWS, LANES))
        near = seen[slab + 1, run].reshape(16 * ROWS, LANES)
        far = seen[slab, run].reshape(16 * ROWS, LANES)
        chosen = jnp.where(lag == 0, near, far)
        high = chosen.astype(jnp.bfloat16)
        rhs[run, :, :LANES] = high
        rhs[run, :, LANES:] = (chosen - high.astype(jnp.float32)).astype(jnp.bfloat16)
        give(slab, run, 0)
        keep(slab, run, 0)
        pass_on(slab, run, 0)
        for group in range(1, AHEAD):
            give(slab, run, group)
        keep(slab, run, 1)

    def give(slab, run, group):
        first, last = GROUPS[group]
        x_send[slab, run, first * ROWS : last * ROWS, :] = product(run, first, last - first)
        if group:
            x_copy(slab, run, group).start()
            return
        for which in (0, 1):
            for way in range(2):
                if pair_offsets(way, run, 0)[which] is not None:
                    d_copy(slab, run, way, which).start()

    def keep(slab, run, group):
        first, last = GROUPS[group]
        own[slab, run, first * ROWS : last * ROWS, :] = product(run, 16 + first, last - first)

    def pair_offsets(way, run, step):
        sign = 1 if way == 0 else -1
        far, near = sign * (8 - 2 * step), sign * (7 - 2 * step)
        return (None if step == 0 and way != run else far), near

    def z_copy(slab, run, way, step, which, piece):
        sign = 1 if way == 0 else -1
        rows = pl.ds((step * 2 + which) * ROWS + piece * PIECE, PIECE)
        at = ((step * 2 + which) * 2 + way) * PIECES + piece
        return pltpu.make_async_remote_copy(
            src_ref=z_send.at[slab, run, way, rows],
            dst_ref=z_recv.at[slab, run, way, rows],
            send_sem=send_sem.at[slab, run],
            recv_sem=z_sem.at[slab, run, at],
            device_id=z_device(sign * (2 - which)),
            device_id_type=MESH,
        )

    def d_copy(slab, run, way, which):
        at = PLACE[pair_offsets(way, run, 0)[which]] * ROWS
        return pltpu.make_async_remote_copy(
            src_ref=x_send.at[slab, run, pl.ds(at, ROWS)],
            dst_ref=d_recv.at[slab, run, pl.ds((way * 2 + which) * ROWS, ROWS)],
            send_sem=send_sem.at[slab, run],
            recv_sem=d_sem.at[slab, run, way * 2 + which],
            device_id=z_device((2 - which) * (1 if way == 0 else -1), True),
            device_id_type=MESH,
        )

    def pass_on(slab, run, step):
        if step:
            x_copy(slab, run, step).wait_recv()
        for which in (1, 0) if step else (0, 1):
            for piece in range(PIECES):
                for way in range(2):
                    offset = pair_offsets(way, run, step)[which]
                    if offset is None:
                        continue
                    at = PLACE[offset] * ROWS + piece * PIECE
                    total = own[slab, run, at : at + PIECE, :]
                    if step:
                        total = total + x_recv[slab, run, at : at + PIECE, :]
                    if step and which == 0:
                        for past in range(2):
                            if pair_offsets(way, run, step - 1)[past] is None:
                                continue
                            z_copy(slab, run, way, step - 1, past, piece).wait_recv()
                            came = ((step - 1) * 2 + past) * ROWS + piece * PIECE
                            total = total + z_recv[slab, run, way, came : came + PIECE, :]
                            if step == 1:
                                d_copy(slab, run, way, past).wait_recv()
                                came = (way * 2 + past) * ROWS + piece * PIECE
                                total = total + d_recv[slab, run, came : came + PIECE, :]
                    to = (step * 2 + which) * ROWS + piece * PIECE
                    z_send[slab, run, way, to : to + PIECE, :] = total
                    z_copy(slab, run, way, step, which, piece).start()
        if step:
            if step + AHEAD - 1 < 5:
                give(slab, run, step + AHEAD - 1)
            keep(slab, run, step + 1)

    def finish(slab, run):
        x_copy(slab, run, 4).wait_recv()
        total = own[slab, run, 15 * ROWS :, :] + x_recv[slab, run, 15 * ROWS :, :]
        for which in range(2):
            for way in range(2):
                for piece in range(PIECES):
                    z_copy(slab, run, way, 3, which, piece).wait_recv()
                came = (6 + which) * ROWS
                total = total + z_recv[slab, run, way, came : came + ROWS, :]
        high = total.astype(jnp.bfloat16)
        low = (total - high.astype(jnp.float32)).astype(jnp.bfloat16)
        filtered = jnp.dot(high, kt_hi[...], preferred_element_type=jnp.float32) + (
            jnp.dot(high, kt_lo[...], preferred_element_type=jnp.float32)
            + jnp.dot(low, kt_hi[...], preferred_element_type=jnp.float32)
        )
        value = filtered + drive_v[slab, pl.ds(run, ROWS, stride=2), :]
        fresh = 1.0 / (1.0 + jnp.exp(-value))
        if slab < SLABS - 1:
            seen[slab + 2, run, chip, core] = fresh
            send_all(slab + 2, run, send_sem.at[slab, run], gather_sem.at[slab + 2, run])
        out[slab, pl.ds(run, ROWS, stride=2), :] = fresh

    stages = []
    for run in range(RUNS):
        line = []
        for slab in range(SLABS):
            line.append(functools.partial(relay, slab, run))
            line.append(functools.partial(multiply, slab, run))
            for step in range(1, 4):
                line.append(functools.partial(pass_on, slab, run, step))
            line.append(functools.partial(finish, slab, run))
        stages.append(line)
    order = []
    for run in range(RUNS):
        for at, stage in enumerate(stages[run]):
            due = at // 6 * SLAB_US + STAGE_US[at % 6] + run * TAU
            order.append((due, run, at, stage))
    for _, _, _, stage in sorted(order, key=lambda entry: entry[:3]):
        stage()

    for run in range(RUNS):
        for slab in range(2):
            sent = w_raw.at[pl.ds(0, 15 * ROWS)]
            pltpu.make_async_copy(sent, sent, first_send_sem.at[slab, run]).wait()
        for slab in range(SLABS):
            blocks = 16 + 15 + (15 if slab < SLABS - 1 else 0)
            sent = w_raw.at[pl.ds(0, blocks * ROWS)]
            pltpu.make_async_copy(sent, sent, send_sem.at[slab, run]).wait()


def per_device(coupling, lag_class, rates_older, rates_newer, drive, syn_kernel):
    f32, bf16 = jnp.float32, jnp.bfloat16
    rates = pl.pallas_call(
        kernel,
        out_shape=pltpu.VMEM((SLABS, 64, LANES), f32),
        in_specs=[
            pl.BlockSpec(memory_space=pl.ANY),
            pl.BlockSpec(memory_space=pl.ANY),
            pl.BlockSpec(memory_space=pl.ANY),
            pl.BlockSpec(memory_space=pl.ANY),
            pl.BlockSpec(memory_space=pl.ANY),
            pl.BlockSpec(memory_space=pl.ANY),
        ],
        out_specs=pl.BlockSpec(memory_space=pltpu.VMEM),
        scratch_shapes=[
            pltpu.VMEM((4096, LANES), f32),
            pltpu.VMEM((1024, 512), bf16),
            pltpu.VMEM((1024, 512), bf16),
            pltpu.VMEM((4, RUNS, 8, 2, ROWS, LANES), f32),
            pltpu.VMEM((RUNS, 512, 2 * LANES), bf16),
            pltpu.VMEM((SLABS, RUNS, 512, LANES), f32),
            pltpu.VMEM((SLABS, RUNS, 512, LANES), f32),
            pltpu.VMEM((SLABS, RUNS, 512, LANES), f32),
            pltpu.VMEM((SLABS, RUNS, 2, 8 * ROWS, LANES), f32),
            pltpu.VMEM((SLABS, RUNS, 2, 8 * ROWS, LANES), f32),
            pltpu.VMEM((SLABS, RUNS, 4 * ROWS, LANES), f32),
            pltpu.VMEM((64, LANES), f32),
            pltpu.VMEM((64, LANES), f32),
            pltpu.VMEM((SLABS, 64, LANES), f32),
            pltpu.VMEM((LANES, LANES), f32),
            pltpu.VMEM((1, 1), jnp.int32),
            pltpu.VMEM((LANES, LANES), bf16),
            pltpu.VMEM((LANES, LANES), bf16),
            pltpu.SemaphoreType.DMA((5,)),
            pltpu.SemaphoreType.DMA((32,)),
            pltpu.SemaphoreType.DMA((4, RUNS)),
            pltpu.SemaphoreType.DMA((4, RUNS)),
            pltpu.SemaphoreType.DMA((SLABS, RUNS, 5)),
            pltpu.SemaphoreType.DMA((SLABS, RUNS, 16 * PIECES)),
            pltpu.SemaphoreType.DMA((SLABS, RUNS, 4)),
            pltpu.SemaphoreType.DMA((SLABS, RUNS)),
            pltpu.SemaphoreType.DMA((2, RUNS)),
        ],
        compiler_params=pltpu.CompilerParams(collective_id=0, has_side_effects=True),
    )(
        coupling.reshape(4096, LANES),
        lag_class,
        rates_older.reshape(64, LANES),
        rates_newer.reshape(64, LANES),
        drive.reshape(SLABS, 64, LANES),
        syn_kernel,
    )
    return rates.reshape(drive.shape)


def solution(mesh):
    return jax.shard_map(
        per_device,
        mesh=mesh,
        in_specs=(
            P("col", "row", None),
            P("col", "row"),
            P("col", "row", None, None, None),
            P("col", "row", None, None, None),
            P(None, "col", "row", None, None, None),
            P(),
        ),
        out_specs=P(None, "col", "row", None, None, None),
        check_vma=False,
    )
```

```python
import functools

import jax
import jax.numpy as jnp
from jax import lax
from jax.experimental import pallas as pl
from jax.experimental.pallas import tpu as pltpu
from jax.sharding import PartitionSpec as P

MESH = pl.DeviceIdType.MESH
N_Z = 16
ROWS = 32
LANES = 128
SLABS = 3
RUNS = 2
TAU = 3.0
STAGE_US = (5.3, 6.5, 9.9, 12.6, 15.3, 18.0)
SLAB_US = 19.5
PIECE = 32
AHEAD = 3

OFFSETS = (8, 7, -7, 6, 5, -6, -5, 4, 3, -4, -3, 2, 1, -2, -1, 0)
PLACE = {offset: place for place, offset in enumerate(OFFSETS)}
PLACE[-8] = PLACE[8]
PIECES = ROWS // PIECE
GROUPS = ((0, 3), (3, 7), (7, 11), (11, 15), (15, 16))


def kernel(
    coupling, lag_class, older, newer, drive, syn_kernel, out,
    w_raw, w_hi, w_lo, seen, rhs, own, x_send, x_recv, z_send, z_recv, d_recv,
    older_v, newer_v, drive_v, syn_v, lag_v, kt_hi, kt_lo,
    load_sem, w_sem, gather_sem, relay_sem, x_sem, z_sem, d_sem, send_sem, first_send_sem,
):
    row, col = lax.axis_index("row"), lax.axis_index("col")
    z, x_lo = row // 2, row % 2
    x_hi, y, core = col // 8, (col // 2) % 4, col % 2

    loads = [
        pltpu.make_async_copy(src, dst, load_sem.at[i])
        for i, (src, dst) in enumerate(
            ((older, older_v), (newer, newer_v), (drive, drive_v), (syn_kernel, syn_v),
             (lag_class, lag_v))
        )
    ]
    for load in loads:
        load.start()

    def z_device(step, across=False):
        x_of = 1 - x_lo if across else x_lo
        return (lax.rem(z + step + N_Z, N_Z) * 2 + x_of, col)

    x_device = (z * 2 + 1 - x_lo, col)
    peers = [
        (row, lax.rem(x_hi + dx, 2) * 8 + lax.rem(y + dy, 4) * 2 + core)
        for dx, dy in ((1, 2), (1, 1), (1, 3), (1, 0), (0, 2), (0, 1), (0, 3))
    ]
    sibling = (row, col + 1 - 2 * core)

    barrier = pltpu.get_barrier_semaphore()
    partners = peers + [sibling, x_device] + [z_device(s) for s in (1, -1, 2, -2)]
    partners += [z_device(s, True) for s in (1, -1, 2, -2)]
    for device in partners:
        pl.semaphore_signal(barrier, inc=1, device_id=device, device_id_type=MESH)

    w_loads = []
    for half in range(2):
        for place, offset in enumerate(OFFSETS):
            x_of = 1 - x_lo if half == 0 else x_lo
            block = lax.rem(z + offset + N_Z, N_Z) * 2 + x_of
            at = half * 16 + place
            w_loads.append(
                pltpu.make_async_copy(
                    coupling.at[pl.ds(pl.multiple_of(block * 128, 128), 128)],
                    w_raw.at[pl.ds(at * 128, 128)],
                    w_sem.at[at],
                )
            )
    for load in w_loads:
        load.start()

    chip = x_hi * 4 + y

    def send_all(slab, run, sem, recv):
        block = seen.at[slab, run, chip, core]
        for device in peers:
            pltpu.make_async_remote_copy(
                src_ref=block, dst_ref=block, send_sem=sem, recv_sem=recv,
                device_id=device, device_id_type=MESH,
            ).start()

    loads[0].wait()
    loads[1].wait()
    for run in range(RUNS):
        seen[0, run, chip, core] = older_v[pl.ds(run, ROWS, stride=2), :]
        seen[1, run, chip, core] = newer_v[pl.ds(run, ROWS, stride=2), :]
    pl.semaphore_wait(barrier, len(partners))
    for run in range(RUNS):
        for slab in (1, 0):
            send_all(slab, run, first_send_sem.at[slab, run], gather_sem.at[slab, run])

    loads[2].wait()
    loads[3].wait()
    loads[4].wait()
    kt = syn_v[...].T
    kt_h = kt.astype(jnp.bfloat16)
    kt_hi[...] = kt_h
    kt_lo[...] = (kt - kt_h.astype(jnp.float32)).astype(jnp.bfloat16)

    for load in w_loads:
        load.wait()

    def split(at, carry):
        rows = pl.ds(pl.multiple_of(at * ROWS, ROWS), ROWS)
        for q in range(4):
            w = w_raw[pl.ds(at * 128 + q, ROWS, stride=4), :]
            w_h = w.astype(jnp.bfloat16)
            w_hi[rows, q * LANES : (q + 1) * LANES] = w_h
            w_lo[rows, q * LANES : (q + 1) * LANES] = (
                w - w_h.astype(jnp.float32)
            ).astype(jnp.bfloat16)
        return carry

    lax.fori_loop(0, 32, split, 0)

    def relay_copy(slab, run):
        blocks = seen.at[slab, run, :, core]
        sem = first_send_sem.at[slab, run] if slab < 2 else send_sem.at[slab - 2, run]
        return pltpu.make_async_remote_copy(
            src_ref=blocks, dst_ref=blocks, send_sem=sem, recv_sem=relay_sem.at[slab, run],
            device_id=sibling, device_id_type=MESH,
        )

    def relay(slab, run):
        for of in (1, 0) if slab == 0 else (slab + 1,):
            rest = seen.at[of, run, pl.ds(0, 7), 0]
            pltpu.make_async_copy(rest, rest, gather_sem.at[of, run]).wait()
            relay_copy(of, run).start()
        prepare(slab, run, core)

    def prepare(slab, run, of_core):
        lag = jnp.broadcast_to(lag_v[...], (8 * ROWS, LANES)).reshape(8, ROWS, LANES)
        chosen = jnp.where(
            lag == 0, seen[slab + 1, run, :, of_core], seen[slab, run, :, of_core]
        )
        high = chosen.astype(jnp.bfloat16)
        rhs[run, :, of_core, :, :LANES] = high
        rhs[run, :, of_core, :, LANES:] = (
            chosen - high.astype(jnp.float32)
        ).astype(jnp.bfloat16)

    def product(run, first, count):
        rows = pl.ds(first * ROWS, count * ROWS)
        right = rhs[run].reshape(16 * ROWS, 2 * LANES)
        both = jnp.dot(w_hi[rows, :], right, preferred_element_type=jnp.float32)
        low = jnp.dot(
            w_lo[rows, :], right[:, :LANES], preferred_element_type=jnp.float32
        )
        return both[:, :LANES] + (both[:, LANES:] + low)

    def x_copy(slab, run, group):
        first, last = GROUPS[group]
        rows = pl.ds(first * ROWS, (last - first) * ROWS)
        return pltpu.make_async_remote_copy(
            src_ref=x_send.at[slab, run, rows],
            dst_ref=x_recv.at[slab, run, rows],
            send_sem=send_sem.at[slab, run],
            recv_sem=x_sem.at[slab, run, group],
            device_id=x_device, device_id_type=MESH,
        )

    def multiply(slab, run):
        if slab == 0:
            relay_copy(0, run).wait_recv()
        relay_copy(slab + 1, run).wait_recv()
        prepare(slab, run, 1 - core)
        give(slab, run, 0)
        keep(slab, run, 0)
        pass_on(slab, run, 0)
        for group in range(1, AHEAD):
            give(slab, run, group)
        keep(slab, run, 1)

    def give(slab, run, group):
        first, last = GROUPS[group]
        x_send[slab, run, first * ROWS : last * ROWS, :] = product(run, first, last - first)
        if group:
            x_copy(slab, run, group).start()
            return
        for which in (0, 1):
            for way in range(2):
                if pair_offsets(way, run, 0)[which] is not None:
                    d_copy(slab, run, way, which).start()

    def keep(slab, run, group):
        first, last = GROUPS[group]
        own[slab, run, first * ROWS : last * ROWS, :] = product(run, 16 + first, last - first)

    def pair_offsets(way, run, step):
        sign = 1 if way == 0 else -1
        far, near = sign * (8 - 2 * step), sign * (7 - 2 * step)
        return (None if step == 0 and way != run else far), near

    def z_copy(slab, run, way, step, which, piece):
        sign = 1 if way == 0 else -1
        rows = pl.ds((step * 2 + which) * ROWS + piece * PIECE, PIECE)
        at = ((step * 2 + which) * 2 + way) * PIECES + piece
        return pltpu.make_async_remote_copy(
            src_ref=z_send.at[slab, run, way, rows],
            dst_ref=z_recv.at[slab, run, way, rows],
            send_sem=send_sem.at[slab, run],
            recv_sem=z_sem.at[slab, run, at],
            device_id=z_device(sign * (2 - which)),
            device_id_type=MESH,
        )

    def d_copy(slab, run, way, which):
        at = PLACE[pair_offsets(way, run, 0)[which]] * ROWS
        return pltpu.make_async_remote_copy(
            src_ref=x_send.at[slab, run, pl.ds(at, ROWS)],
            dst_ref=d_recv.at[slab, run, pl.ds((way * 2 + which) * ROWS, ROWS)],
            send_sem=send_sem.at[slab, run],
            recv_sem=d_sem.at[slab, run, way * 2 + which],
            device_id=z_device((2 - which) * (1 if way == 0 else -1), True),
            device_id_type=MESH,
        )

    def pass_on(slab, run, step):
        if step:
            x_copy(slab, run, step).wait_recv()
        for which in (1, 0) if step else (0, 1):
            for piece in range(PIECES):
                for way in range(2):
                    offset = pair_offsets(way, run, step)[which]
                    if offset is None:
                        continue
                    at = PLACE[offset] * ROWS + piece * PIECE
                    total = own[slab, run, at : at + PIECE, :]
                    if step:
                        total = total + x_recv[slab, run, at : at + PIECE, :]
                    if step and which == 0:
                        for past in range(2):
                            if pair_offsets(way, run, step - 1)[past] is None:
                                continue
                            z_copy(slab, run, way, step - 1, past, piece).wait_recv()
                            came = ((step - 1) * 2 + past) * ROWS + piece * PIECE
                            total = total + z_recv[slab, run, way, came : came + PIECE, :]
                            if step == 1:
                                d_copy(slab, run, way, past).wait_recv()
                                came = (way * 2 + past) * ROWS + piece * PIECE
                                total = total + d_recv[slab, run, came : came + PIECE, :]
                    to = (step * 2 + which) * ROWS + piece * PIECE
                    z_send[slab, run, way, to : to + PIECE, :] = total
                    z_copy(slab, run, way, step, which, piece).start()
        if step:
            if step + AHEAD - 1 < 5:
                give(slab, run, step + AHEAD - 1)
            keep(slab, run, step + 1)

    def finish(slab, run):
        x_copy(slab, run, 4).wait_recv()
        total = own[slab, run, 15 * ROWS :, :] + x_recv[slab, run, 15 * ROWS :, :]
        for which in range(2):
            for way in range(2):
                for piece in range(PIECES):
                    z_copy(slab, run, way, 3, which, piece).wait_recv()
                came = (6 + which) * ROWS
                total = total + z_recv[slab, run, way, came : came + ROWS, :]
        high = total.astype(jnp.bfloat16)
        low = (total - high.astype(jnp.float32)).astype(jnp.bfloat16)
        filtered = jnp.dot(high, kt_hi[...], preferred_element_type=jnp.float32) + (
            jnp.dot(high, kt_lo[...], preferred_element_type=jnp.float32)
            + jnp.dot(low, kt_hi[...], preferred_element_type=jnp.float32)
        )
        value = filtered + drive_v[slab, pl.ds(run, ROWS, stride=2), :]
        fresh = 1.0 / (1.0 + jnp.exp(-value))
        if slab < SLABS - 1:
            seen[slab + 2, run, chip, core] = fresh
            send_all(slab + 2, run, send_sem.at[slab, run], gather_sem.at[slab + 2, run])
        out[slab, pl.ds(run, ROWS, stride=2), :] = fresh

    stages = []
    for run in range(RUNS):
        line = []
        for slab in range(SLABS):
            line.append(functools.partial(relay, slab, run))
            line.append(functools.partial(multiply, slab, run))
            for step in range(1, 4):
                line.append(functools.partial(pass_on, slab, run, step))
            line.append(functools.partial(finish, slab, run))
        stages.append(line)
    order = []
    for run in range(RUNS):
        for at, stage in enumerate(stages[run]):
            due = at // 6 * SLAB_US + STAGE_US[at % 6] + run * TAU
            order.append((due, run, at, stage))
    for _, _, _, stage in sorted(order, key=lambda entry: entry[:3]):
        stage()

    for run in range(RUNS):
        for slab in range(2):
            sent = w_raw.at[pl.ds(0, 15 * ROWS)]
            pltpu.make_async_copy(sent, sent, first_send_sem.at[slab, run]).wait()
        for slab in range(SLABS):
            blocks = 16 + 15 + (15 if slab < SLABS - 1 else 0)
            sent = w_raw.at[pl.ds(0, blocks * ROWS)]
            pltpu.make_async_copy(sent, sent, send_sem.at[slab, run]).wait()


def per_device(coupling, lag_class, rates_older, rates_newer, drive, syn_kernel):
    f32, bf16 = jnp.float32, jnp.bfloat16
    rates = pl.pallas_call(
        kernel,
        out_shape=pltpu.VMEM((SLABS, 64, LANES), f32),
        in_specs=[
            pl.BlockSpec(memory_space=pl.ANY),
            pl.BlockSpec(memory_space=pl.ANY),
            pl.BlockSpec(memory_space=pl.ANY),
            pl.BlockSpec(memory_space=pl.ANY),
            pl.BlockSpec(memory_space=pl.ANY),
            pl.BlockSpec(memory_space=pl.ANY),
        ],
        out_specs=pl.BlockSpec(memory_space=pltpu.VMEM),
        scratch_shapes=[
            pltpu.VMEM((4096, LANES), f32),
            pltpu.VMEM((1024, 512), bf16),
            pltpu.VMEM((1024, 512), bf16),
            pltpu.VMEM((4, RUNS, 8, 2, ROWS, LANES), f32),
            pltpu.VMEM((RUNS, 8, 2, ROWS, 2 * LANES), bf16),
            pltpu.VMEM((SLABS, RUNS, 512, LANES), f32),
            pltpu.VMEM((SLABS, RUNS, 512, LANES), f32),
            pltpu.VMEM((SLABS, RUNS, 512, LANES), f32),
            pltpu.VMEM((SLABS, RUNS, 2, 8 * ROWS, LANES), f32),
            pltpu.VMEM((SLABS, RUNS, 2, 8 * ROWS, LANES), f32),
            pltpu.VMEM((SLABS, RUNS, 4 * ROWS, LANES), f32),
            pltpu.VMEM((64, LANES), f32),
            pltpu.VMEM((64, LANES), f32),
            pltpu.VMEM((SLABS, 64, LANES), f32),
            pltpu.VMEM((LANES, LANES), f32),
            pltpu.VMEM((1, 1), jnp.int32),
            pltpu.VMEM((LANES, LANES), bf16),
            pltpu.VMEM((LANES, LANES), bf16),
            pltpu.SemaphoreType.DMA((5,)),
            pltpu.SemaphoreType.DMA((32,)),
            pltpu.SemaphoreType.DMA((4, RUNS)),
            pltpu.SemaphoreType.DMA((4, RUNS)),
            pltpu.SemaphoreType.DMA((SLABS, RUNS, 5)),
            pltpu.SemaphoreType.DMA((SLABS, RUNS, 16 * PIECES)),
            pltpu.SemaphoreType.DMA((SLABS, RUNS, 4)),
            pltpu.SemaphoreType.DMA((SLABS, RUNS)),
            pltpu.SemaphoreType.DMA((2, RUNS)),
        ],
        compiler_params=pltpu.CompilerParams(collective_id=0, has_side_effects=True),
    )(
        coupling.reshape(4096, LANES),
        lag_class,
        rates_older.reshape(64, LANES),
        rates_newer.reshape(64, LANES),
        drive.reshape(SLABS, 64, LANES),
        syn_kernel,
    )
    return rates.reshape(drive.shape)


def solution(mesh):
    return jax.shard_map(
        per_device,
        mesh=mesh,
        in_specs=(
            P("col", "row", None),
            P("col", "row"),
            P("col", "row", None, None, None),
            P("col", "row", None, None, None),
            P(None, "col", "row", None, None, None),
            P(),
        ),
        out_specs=P(None, "col", "row", None, None, None),
        check_vma=False,
    )
```
